128 devices in a mesh: row: 8 (over y, core), col: 16 (over z, x).
Axes of the slice: x: 4, y: 4, z: 4, core: 2. Of those that a mesh axis runs over, the one named last changes fastest.
Arguments:
- trailing_inverse: float32 [24576, 24576], P('row', 'col'), may hold values from -6 to 6
- factor_cols: float32 [3, 24576, 256], P(None, ('col', 'row')), may hold values from -0.0390625 to 0.0390625
- factor_blocks: float32 [3, 256, 256], replicated, may hold values from -0.375 to 0.375
- diag_inverse: float32 [3, 256, 256], replicated, may hold values from -6 to 6
Outputs:
- inv_cols: float32 [3, 24576, 256], P(None, ('row', 'col'))
- inv_diag: float32 [3, 256, 256], replicated
- inv_cross: float32 [3, 256, 256], replicated
The draws below stay inside these ranges and needn't reach their ends.
All inputs are finite; a program needn't handle non-finite values.
Results may differ from the reference program's by a relative error of at most 0.0001.
Values sent between devices are 32-bit elements; how exact they have to be, the bound alone decides.
No kernel may reach another device: no remote copies, remote signals or barrier semaphores. Data moves between devices by JAX's collectives and lax.ppermute only.
A program may use at most 128 MiB of HBM per device.

```python
import jax
import jax.numpy as jnp
from jax import lax

W = 256
NS = 3
R = 24576
NPAIR = 3


def levels(own_key, shape, cuts, low, largest):
    gain = 1.0
    for axis_at, parts in cuts:
        draws = jax.random.uniform(jax.random.fold_in(jax.random.fold_in(own_key, 6), axis_at), (parts,), jnp.float32, low / len(cuts), largest / len(cuts))
        gain = gain * jnp.repeat(jnp.exp(draws), shape[axis_at] // parts).reshape((-1,) + (1,) * (len(shape) - 1 - axis_at))
    return gain


def bell_draw(key, extent, spread, limit, shards=(), dtype=jnp.bfloat16):
    array = spread * jax.random.normal(key, extent, jnp.float32)
    if shards:
        array = array * levels(key, extent, shards, -0.22, 0.18)
    return jnp.clip(array, -limit, limit).astype(dtype)


def setup_inputs(seed: int = 0) -> dict:
    key_list = jax.random.split(jax.random.key(seed), 5)
    trailing_inverse = bell_draw(key_list[0], (R, R), 1.0, 6.0, ((0, 8), (1, 16)), jnp.float32)
    factor_cols = bell_draw(key_list[1], (NS, R, W), R ** -0.5, 0.0390625, ((1, 128),), jnp.float32)
    factor_blocks = bell_draw(key_list[2], (NPAIR, W, W), W ** -0.5, 0.375, (), jnp.float32)
    diag_inverse = bell_draw(key_list[3], (NS, W, W), 1.0, 6.0, (), jnp.float32)
    return dict(trailing_inverse=trailing_inverse, factor_cols=factor_cols, factor_blocks=factor_blocks, diag_inverse=diag_inverse)


def product(left, right):
    return jnp.dot(left, right, precision=lax.Precision.HIGHEST, preferred_element_type=jnp.float32)


def pair_order(node_count):
    return [(later_node, target_node) for target_node in reversed(range(node_count)) for later_node in range(target_node + 1, node_count)]


def reference(trailing_inverse, factor_cols, factor_blocks, diag_inverse):
    node_count = factor_cols.shape[0]
    pair_list = pair_order(node_count)
    columns = [None] * node_count
    blocks = {}
    for target_node in reversed(range(node_count)):
        accumulated = product(trailing_inverse, factor_cols[target_node])
        for later_node in range(target_node + 1, node_count):
            accumulated = accumulated + product(columns[later_node], factor_blocks[pair_list.index((later_node, target_node))])
        columns[target_node] = -accumulated
        for later_node in range(target_node + 1, node_count):
            value_sum = product(columns[later_node].T, factor_cols[target_node])
            for other_node in range(target_node + 1, node_count):
                if later_node >= other_node:
                    block_value = blocks[(later_node, other_node)]
                else:
                    block_value = blocks[(other_node, later_node)].T
                value_sum = value_sum + product(block_value, factor_blocks[pair_list.index((other_node, target_node))])
            blocks[(later_node, target_node)] = -value_sum
        diag_term = product(factor_cols[target_node].T, columns[target_node])
        for later_node in range(target_node + 1, node_count):
            diag_term = diag_term + product(factor_blocks[pair_list.index((later_node, target_node))].T, blocks[(later_node, target_node)])
        blocks[(target_node, target_node)] = diag_inverse[target_node] - diag_term
    inv_cols = jnp.stack(columns)
    inv_diag = jnp.stack([blocks[(node_index, node_index)] for node_index in range(node_count)])
    inv_cross = jnp.stack([blocks[slot_pair] for slot_pair in pair_list])
    return (inv_cols, inv_diag, inv_cross)
```

```python
import functools

import jax
import jax.numpy as jnp
from jax import lax
from jax.experimental import pallas as pl
from jax.experimental.pallas import tpu as pltpu
from jax.sharding import PartitionSpec as P


F32 = jnp.float32
BF16 = jnp.bfloat16
AXES = ("row", "col")


def device_index(y, core, z, x):
    return ((y % 4) * 2 + core) * 16 + (z % 4) * 4 + (x % 4)


def pairs(move):
    return [
        (device_index(y, core, z, x), device_index(*move(y, core, z, x)))
        for y in range(4)
        for core in range(2)
        for z in range(4)
        for x in range(4)
    ]


SWAP = pairs(lambda y, c, z, x: (y, 1 - c, z, x))


def along_y(step):
    return pairs(lambda y, c, z, x: (y + step, c, z, x))


FORWARD = pairs(lambda y, c, z, x: (y + (1 if c == 0 else -1), c, z, x))


def first_stage(step):
    return pairs(lambda y, c, z, x: (y, c, z, x + step) if c == 0 else (y, c, z + step, x))


def second_stage(step):
    return pairs(lambda y, c, z, x: (y, c, z + step, x) if c == 0 else (y, c, z, x + step))


def move(value, perm):
    return lax.ppermute(value, AXES, perm)


def split(value):
    high = value.astype(BF16)
    low = (value - high.astype(F32)).astype(BF16)
    return high, low


def exact(left, right, contract=((1,), (0,))):
    return lax.dot_general(
        left, right, (contract, ((), ())), precision=lax.Precision.HIGHEST, preferred_element_type=F32
    )


def in_vmem(shape, dtype):
    return pltpu.VMEM(shape, dtype)


WHOLE = pl.BlockSpec(memory_space=pltpu.VMEM)
SCALARS = pl.BlockSpec(memory_space=pltpu.SMEM)
SMALL = pltpu.CompilerParams(vmem_limit_bytes=8 << 20)


def pack_kernel(steps, filled, s_ref, *refs):
    pieces, high_ref, low_ref = refs[: len(steps)], refs[-2], refs[-1]
    y, core = s_ref[3], s_ref[0]
    for piece, (step, other) in zip(pieces, steps):
        nodes, rows, width = piece.shape
        owner = 1 - core if other else core
        at = pl.multiple_of((lax.rem(y + step + 4, 4) * 2 + owner) * rows, rows)
        for node in range(nodes):
            high, low = split(piece[node])
            high_ref[pl.ds(at, rows), node * width : (node + 1) * width] = high
            low_ref[pl.ds(at, rows), node * width : (node + 1) * width] = low


def pack(scalars, pieces, steps, filled=None):
    nodes, rows, width = pieces[0].shape
    shape = in_vmem((8 * rows, nodes * width), BF16)
    count = len(pieces)
    filled = list(filled) if filled else []
    return pl.pallas_call(
        functools.partial(pack_kernel, steps, filled),
        out_shape=(shape, shape),
        in_specs=[SCALARS] + [WHOLE] * (count + len(filled)),
        out_specs=(WHOLE, WHOLE),
        input_output_aliases={1 + count: 0, 2 + count: 1} if filled else {},
        compiler_params=SMALL,
        name="pack",
    )(scalars, *pieces, *filled)


def halve_kernel(t_ref, high_ref, low_ref):
    step = pl.program_id(0)
    outer, inner = step // 4, step % 4
    for half, (first, second) in enumerate(((inner, outer), (4 + outer, inner))):
        high, low = split(t_ref[half])
        high_ref[first, second] = high
        low_ref[first, second] = low


def halve(blocks):
    count, rows, depth = blocks.shape
    shape = in_vmem((8, 4, rows, depth), BF16)
    return pl.pallas_call(
        halve_kernel,
        out_shape=(shape, shape),
        grid=(count // 2,),
        in_specs=[pl.BlockSpec((2, rows, depth), lambda j: (j, 0, 0))],
        out_specs=(WHOLE, WHOLE),
        compiler_params=SMALL,
        name="halve",
    )(blocks)


def product_kernel(side, step, add, s_ref, th_ref, tl_ref, fh_ref, fl_ref, *rest):
    out_ref = rest[-1]
    core, z, x = s_ref[0], s_ref[1], s_ref[2]
    half = core if side == 0 else 1 - core
    group = jnp.where(half == 0, lax.rem(x + step % 4, 4), 4 + lax.rem(z + step % 4, 4))
    rows, depth = th_ref.shape[2:]
    columns = fh_ref.shape[1]
    for start in range(0, columns, 256):
        cut = slice(start, start + 256)
        high = th_ref[group].reshape(4 * rows, depth)
        low = tl_ref[group].reshape(4 * rows, depth)
        value = jnp.dot(high, fh_ref[:, cut], preferred_element_type=F32)
        value = value + jnp.dot(high, fl_ref[:, cut], preferred_element_type=F32)
        value = value + jnp.dot(low, fh_ref[:, cut], preferred_element_type=F32)
        value = value.reshape(4, rows, 256)
        if add:
            value = value + rest[0][:, :, cut]
        out_ref[:, :, cut] = value


def product(scalars, halves, factors, side, step, addend=None):
    rows, depth = halves[0].shape[2:]
    columns = factors[0].shape[1]
    extra = [] if addend is None else [addend]
    return pl.pallas_call(
        functools.partial(product_kernel, side, step, addend is not None),
        out_shape=in_vmem((4, rows, columns), F32),
        in_specs=[SCALARS] + [WHOLE] * (4 + len(extra)),
        out_specs=WHOLE,
        compiler_params=SMALL,
        cost_estimate=pl.CostEstimate(
            flops=2 * 3 * 4 * rows * depth * columns, bytes_accessed=0, transcendentals=0
        ),
        name="product",
    )(scalars, *halves, *factors, *extra)


def tail_kernel(s_ref, mine_ref, got_ref, rows_ref, blocks_ref, cols_ref, keep_ref, give_ref, own):
    core = s_ref[0]
    half = mine_ref.shape[0]
    own[pl.ds(pl.multiple_of(core * half, half), half), :] = mine_ref[...]
    own[pl.ds(pl.multiple_of((1 - core) * half, half), half), :] = got_ref[...]
    width = blocks_ref.shape[1]
    l21, l10, l20 = blocks_ref[0], blocks_ref[1], blocks_ref[2]
    c2 = -own[:, 2 * width :]
    c1 = -(own[:, width : 2 * width] + exact(c2, l21))
    c0 = -(own[:, :width] + exact(c1, l10) + exact(c2, l20))
    cols_ref[0], cols_ref[1], cols_ref[2] = c0, c1, c2
    f0, f1, f2 = rows_ref[0], rows_ref[1], rows_ref[2]
    down = ((0,), (0,))
    terms = (
        exact(f2, c2, down),
        exact(c2, f1, down),
        exact(f1, c1, down),
        exact(c1, f0, down),
        exact(c2, f0, down),
        exact(f0, c0, down),
    )
    for slot, term in enumerate(terms):
        side, at = slot // 3, slot % 3 * 512

        @pl.when(core == side)
        def _():
            keep_ref[at : at + 256] = term[:, :128]
            keep_ref[at + 256 : at + 512] = term[:, 128:]

        @pl.when(core != side)
        def _():
            give_ref[at : at + 256] = term[:, :128]
            give_ref[at + 256 : at + 512] = term[:, 128:]


def tail(scalars, mine, got, rows, blocks):
    half, columns = mine.shape
    whole2 = lambda j, s: (0, 0)
    whole3 = lambda j, s: (0, 0, 0)
    part = jax.ShapeDtypeStruct((1536, 128), F32)
    return pl.pallas_call(
        tail_kernel,
        out_shape=(jax.ShapeDtypeStruct(rows.shape, F32), part, part),
        grid_spec=pltpu.PrefetchScalarGridSpec(
            num_scalar_prefetch=1,
            grid=(1,),
            in_specs=[
                pl.BlockSpec(mine.shape, whole2),
                pl.BlockSpec(got.shape, whole2),
                pl.BlockSpec(rows.shape, whole3),
                pl.BlockSpec(blocks.shape, whole3),
            ],
            out_specs=[
                pl.BlockSpec(rows.shape, whole3),
                pl.BlockSpec((1536, 128), whole2),
                pl.BlockSpec((1536, 128), whole2),
            ],
            scratch_shapes=[pltpu.VMEM((2 * half, columns), F32)],
        ),
        name="tail",
    )(scalars, mine, got, rows, blocks)


def finish_kernel(s_ref, mine_ref, got_ref, blocks_ref, diag_ref, inv_diag_ref, inv_cross_ref, sums):
    core = s_ref[0]
    sums[pl.ds(pl.multiple_of(core * 1536, 1536), 1536), :] = mine_ref[...]
    sums[pl.ds(pl.multiple_of((1 - core) * 1536, 1536), 1536), :] = got_ref[...]

    def total(slot):
        at = slot * 512
        return jnp.concatenate([sums[at : at + 256], sums[at + 256 : at + 512]], axis=1)

    l21, l10, l20 = blocks_ref[0], blocks_ref[1], blocks_ref[2]
    down = ((0,), (0,))
    b22 = diag_ref[2] - total(0)
    b21 = -(total(1) + exact(b22, l21))
    b11 = diag_ref[1] - (total(2) + exact(l21, b21, down))
    b10 = -(total(3) + exact(b11, l10) + exact(b21, l20, down))
    b20 = -(total(4) + exact(b21, l10) + exact(b22, l20))
    b00 = diag_ref[0] - (total(5) + exact(l10, b10, down) + exact(l20, b20, down))
    inv_diag_ref[0], inv_diag_ref[1], inv_diag_ref[2] = b00, b11, b22
    inv_cross_ref[0], inv_cross_ref[1], inv_cross_ref[2] = b21, b10, b20


def finish(scalars, mine, got, blocks, diag):
    whole2 = lambda j, s: (0, 0)
    whole3 = lambda j, s: (0, 0, 0)
    shape = jax.ShapeDtypeStruct(diag.shape, F32)
    return pl.pallas_call(
        finish_kernel,
        out_shape=(shape, shape),
        grid_spec=pltpu.PrefetchScalarGridSpec(
            num_scalar_prefetch=1,
            grid=(1,),
            in_specs=[
                pl.BlockSpec(mine.shape, whole2),
                pl.BlockSpec(got.shape, whole2),
                pl.BlockSpec(blocks.shape, whole3),
                pl.BlockSpec(diag.shape, whole3),
            ],
            out_specs=[pl.BlockSpec(diag.shape, whole3)] * 2,
            scratch_shapes=[pltpu.VMEM((3072, 128), F32)],
        ),
        name="finish",
    )(scalars, mine, got, blocks, diag)


def own_rows_pairs():
    found = []
    for row in range(8):
        for col in range(16):
            block = col * 8 + row
            found.append((row * 16 + col, (block // 16) * 16 + block % 16))
    return found


CORE_GROUPS = [
    [device_index(y, core, z, x) for y in range(4) for z in range(4) for x in range(4)] for core in range(2)
]


def exchange(value):
    return lax.all_to_all(
        value, AXES, split_axis=0, concat_axis=0, tiled=True, axis_index_groups=CORE_GROUPS
    )


def per_device(trailing_inverse, factor_cols, factor_blocks, diag_inverse):
    row_index, col_index = lax.axis_index("row"), lax.axis_index("col")
    core, y = row_index % 2, row_index // 2
    z, x = col_index // 4, col_index % 4
    scalars = jnp.stack([core, z, x, y]).astype(jnp.int32)
    depth = trailing_inverse.shape[1]
    blocks = trailing_inverse.reshape(32, trailing_inverse.shape[0] // 32, depth)

    below = move(factor_cols, along_y(1))
    above = move(factor_cols, along_y(-1))
    far = move(jnp.where(core == 0, below, above), FORWARD)
    own_factor = move(factor_cols, own_rows_pairs())
    halves = halve(blocks)
    near = [factor_cols, below, above]
    near += [move(piece, SWAP) for piece in near]
    factors = pack(scalars, near, tuple((step, other) for other in (False, True) for step in (0, -1, 1)))
    factors = pack(scalars, [far, move(far, SWAP)], ((2, False), (2, True)), factors)

    ahead, back = first_stage(1), first_stage(-1)
    times = functools.partial(product, scalars, halves, factors)
    mine, give = 0, 1
    give_far = move(times(give, 2), SWAP)
    sum_ahead = move(times(mine, 2), ahead)
    sum_back = move(give_far, back)
    got_ahead = move(move(times(give, 1), SWAP), ahead)
    mine_back = move(times(mine, -1), back)
    got_near = move(times(give, -1), SWAP)
    mine_ahead = move(times(mine, 1, sum_ahead), ahead)
    got_back = move(got_near + sum_back, back)
    got_own = move(times(give, 0), SWAP)
    mine_own = times(mine, 0)

    at = jnp.where(core == 0, z, x)

    def total(values, step):
        parts = [lax.dynamic_index_in_dim(value, (at + step) % 4, 0, keepdims=False) for value in values]
        return parts[0] + parts[1] + parts[2]

    mine = functools.partial(total, (mine_own, mine_ahead, mine_back))
    got = functools.partial(total, (got_own, got_ahead, got_back))
    ahead, back = second_stage(1), second_stage(-1)
    low_sum_ahead = move(mine(2), ahead)
    low_sum_back = move(got(2), back)
    low_got_ahead = move(got(1), ahead)
    low_mine_back = move(mine(3), back)
    low_mine_ahead = move(mine(1) + low_sum_ahead, ahead)
    low_got_back = move(got(3) + low_sum_back, back)
    mine_half = mine(0) + low_mine_ahead + low_mine_back
    got_half = move(got(0) + low_got_ahead + low_got_back, SWAP)

    inv_cols, keep, give = tail(scalars, mine_half, got_half, own_factor, factor_blocks)
    received = exchange(keep + move(give, SWAP))
    summed = received.reshape(64, 24, 128).sum(0)
    spread = jnp.broadcast_to(summed[None], (64, 24, 128)).reshape(1536, 128)
    gathered = exchange(spread)
    inv_diag, inv_cross = finish(scalars, gathered, move(gathered, SWAP), factor_blocks, diag_inverse)
    return (inv_cols, inv_diag, inv_cross)


def solution(mesh):
    return jax.shard_map(
        per_device,
        mesh=mesh,
        in_specs=(P("row", "col"), P(None, ("col", "row"), None), P(), P()),
        out_specs=(P(None, ("row", "col"), None), P(), P()),
        check_vma=False,
    )
```
